32 devices in a mesh: grp: 2 (over y), field: 4 (over z), pair: 4 (over x, core).
Axes of the slice: x: 2, y: 2, z: 4, core: 2. Of those that a mesh axis runs over, the one named last changes fastest.
Arguments:
- cholesky_tensor: float32 [1536, 9216], P(('grp', 'field'), 'pair'), parts along dimension 0, may hold values from -0.0625 to 0.0625
- green_function: float32 [2, 8192, 9216], P(None, ('grp', 'field'), 'pair'), parts along dimension 1, may hold values from -6 to 6
- mean_field: float32 [2, 1536], P(None, 'grp'), parts along dimension 1, may hold values from -6 to 6
- field_noise: float32 [8192, 768], P(('grp', 'field')), parts along dimension 0, may hold values from -6 to 6
Outputs:
- capped_bias: float32 [2, 8192, 768], P(None, ('grp', 'field', 'pair')), parts along dimension 1
- one_body: float32 [8192, 2, 9216], P(('grp', 'field'), None, 'pair'), parts along dimension 0
The draws below stay inside these ranges and needn't reach their ends.
There are 2 independent parts, one for each index of `grp`. The reference program is written for one: setup_inputs(seed, part) draws one part's arguments, and reference() takes and returns one part's arrays. A program takes and returns all parts, laid end to end along the dimension named above; each array names one. Nothing has to cross between parts.
All inputs are finite; a program needn't handle non-finite values.
Results may differ from the reference program's by a relative error of at most 0.000059.
Values sent between devices are 32-bit elements; how exact they have to be, the bound alone decides.
A program may use at most 128 MiB of HBM per device.

```python
import math
import jax
import jax.numpy as jnp
from jax import lax

NF = 768
NP = 9216
WALK = 4096


def steps_of(own_key, extent, cuts, least, largest):
    loudness, own = 1.0, jax.random.fold_in(own_key, 6)
    for dim, blocks in cuts:
        draws = jnp.exp(jax.random.uniform(jax.random.fold_in(own, dim), (blocks,), jnp.float32, least / len(cuts), largest / len(cuts)))
        loudness = loudness * jnp.repeat(draws, extent[dim] // blocks).reshape([-1 if axis == dim else 1 for axis in range(len(extent))])
    return loudness


def noise(own_key, dims, deviation, bound, shards=(), kind=jnp.bfloat16):
    factor_of = steps_of(own_key, dims, shards, -0.22, 0.18) if shards else 1.0
    drawn = jax.random.normal(own_key, dims, jnp.float32) * deviation * factor_of
    return jnp.minimum(jnp.maximum(drawn, -bound), bound).astype(kind)


def setup_inputs(seed: int = 0, part: int = 0) -> dict:
    keys = jax.random.split(jax.random.key(seed), 5)
    own_keys = jax.random.split(jax.random.fold_in(keys[4], part), 5)
    cholesky_tensor = noise(own_keys[0], (NF, NP), NP ** -0.5, 0.0625, ((0, 4), (1, 4)), jnp.float32)
    green_function = noise(own_keys[1], (2, WALK, NP), 1.0, 6.0, ((1, 4), (2, 4)), jnp.float32)
    mean_field = noise(own_keys[2], (2, NF), 1.0, 6.0, (), jnp.float32)
    field_noise = noise(own_keys[3], (WALK, NF), 1.0, 6.0, ((0, 4),), jnp.float32)
    return {"cholesky_tensor": cholesky_tensor, "green_function": green_function, "mean_field": mean_field, "field_noise": field_noise}


def reference(cholesky_tensor, green_function, mean_field, field_noise):
    bias = jnp.einsum('cwp,fp->cwf', green_function, cholesky_tensor, precision=lax.Precision.HIGHEST)
    shifted = bias - mean_field[:, None, :]
    capped = 2.0 * jnp.tanh(shifted / 2.0)
    fields = jnp.stack([field_noise - capped[0], -capped[1]], axis=1)
    operator_scale = math.sqrt(NP / NF)
    one_body = operator_scale * jnp.einsum('wcf,fp->wcp', fields, cholesky_tensor, precision=lax.Precision.HIGHEST)
    return (capped, one_body)
```

```python
import functools
import math

import jax
import jax.numpy as jnp
from jax import lax
from jax.experimental import pallas as pl
from jax.experimental.pallas import tpu as pltpu
from jax.sharding import PartitionSpec as P

LANES = 128


def split(x):
    high = x.astype(jnp.bfloat16)
    return high, (x - high.astype(jnp.float32)).astype(jnp.bfloat16)


MESH = pl.DeviceIdType.MESH


def stacked(right, granules, column):
    wide = right[:granules, :, :, column]
    high = right[:granules, 0, :, column]
    return jnp.concatenate([wide.reshape(-1, wide.shape[3]), high.reshape(-1, high.shape[2])], axis=0)


def bias_kernel(
    n_field, n_pair, late, chol_in, green, noise, mean_ref, share_ref, chol_out, capped_out, early_out,
    stack, green_split, staging, right, part, first, second, capped, mean_turned, noise_tile, left,
    ring_send, ring_recv, part_send, part_recv, sum_send, sum_recv, own_send, own_recv,
    peer_send, peer_recv, pass_send, pass_recv, load_sem, green_sem, chol_sem, capped_sem, noise_sem, early_sem,
):
    fields, pairs = stack.shape
    share, slots = share_ref.shape[1], staging.shape[0]
    block = chol_in.shape[0]
    chunk = math.gcd(block, LANES)
    chunks, own = fields // chunk, block // chunk
    granules, per_granule = fields // LANES, LANES // chunk
    half = n_pair // 2
    me_field, me_pair = lax.axis_index("field"), lax.axis_index("pair")
    left_id = {"field": lax.rem(me_field + n_field - 1, n_field)}
    right_id = {"field": lax.rem(me_field + 1, n_field)}
    core, hop = lax.rem(me_pair, 2), me_pair // 2
    partner_id = {"pair": me_pair + 1 - 2 * core}

    def peer_hop(d):
        return lax.rem(hop + d, half)

    def peer_id(d):
        return {"pair": 2 * peer_hop(d) + core}

    barrier = pltpu.get_barrier_semaphore()
    others = [left_id, right_id, partner_id] + [peer_id(d) for d in range(1, half)]
    for other in others:
        pl.semaphore_signal(barrier, inc=1, device_id=other, device_id_type=MESH)
    pl.semaphore_wait(barrier, len(others))

    def remote(source, target, send, recv, device):
        return pltpu.make_async_remote_copy(
            src_ref=source, dst_ref=target, send_sem=send, recv_sem=recv, device_id=device, device_id_type=MESH
        )

    def ring(k):
        source = chol_in.at[pl.ds(k * chunk, chunk)] if k < own else stack.at[pl.ds(k * chunk, chunk)]
        target = stack.at[pl.ds((k + own) * chunk, chunk)]
        return remote(source, target, ring_send.at[k], ring_recv.at[k + own], left_id)

    for k in range(min(own, chunks - own)):
        ring(k).start()
    load = pltpu.make_async_copy(chol_in, stack.at[pl.ds(0, block)], load_sem)
    load.start()
    early = granules - late
    turn = lax.rem(fields - me_field * block, fields)

    def noise_copy(j):
        return pltpu.make_async_copy(noise.at[pl.ds(j * share, share)], noise_tile, noise_sem)

    noise_copy(0).start()
    mean_turned[...] = pltpu.roll(mean_ref[...], turn, 1)

    def fetch(t):
        j, c = t // 2, t % 2
        return pltpu.make_async_copy(green.at[c, pl.ds(j * share, share)], staging.at[t % slots], green_sem.at[t % slots])

    for t in range(slots - 1):
        fetch(t).start()
    for t in range(2 * n_pair):
        if t + slots - 1 < 2 * n_pair:
            fetch(t + slots - 1).start()
        fetch(t).wait()

        @pl.loop(0, share // 16)
        def _(step):
            at = pl.multiple_of(step * 16, 16)
            high, low = split(staging[t % slots, pl.ds(at, 16), :])
            into = pl.multiple_of(t * share + at, 16)
            green_split[pl.ds(into, 16), :pairs] = high
            green_split[pl.ds(into, 16), pairs:] = low

    load.wait()

    def part_copy(g):
        return remote(part.at[g, 1 - core], first.at[g], part_send.at[g], part_recv.at[g], partner_id)

    def sum_copy(g, d):
        source = part.at[g, core, peer_hop(d)]
        return remote(source, second.at[g, d - 1], sum_send.at[g, d - 1], sum_recv.at[g, d - 1], peer_id(d))

    def own_copy(g):
        at = capped.at[g, core, hop]
        return remote(at, at, own_send.at[g], own_recv.at[g], partner_id)

    def peer_copy(g, d):
        at = capped.at[g, core, hop]
        return remote(at, at, peer_send.at[g, d - 1], peer_recv.at[g, d - 1], peer_id(d))

    def pass_copy(g, d):
        at = capped.at[g, core, peer_hop(half - d)]
        return remote(at, at, pass_send.at[g, d - 1], pass_recv.at[g, d - 1], partner_id)

    def chol_copy(g):
        return pltpu.make_async_copy(right.at[g], chol_out.at[g - early], chol_sem.at[g - early])

    def capped_copy(g):
        return pltpu.make_async_copy(capped.at[g], capped_out.at[g - early], capped_sem.at[g - early])

    def products(g):
        for k in range(g * per_granule, (g + 1) * per_granule):
            if k >= own:
                ring(k - own).wait_recv()
                if k + own < chunks:
                    ring(k).start()
        step_rows = 32
        for at in range(0, LANES, step_rows):
            high, low = split(stack[g * LANES + at : g * LANES + at + step_rows, :])
            right[g, 0, at : at + step_rows, :] = high
            right[g, 1, at : at + step_rows, :] = low
        if g >= early:
            chol_copy(g).start()

        def product(side, at):
            rows = pl.ds(pl.multiple_of((2 * at + side) * 2 * share, 16), 2 * share)
            dims = (((1,), (1,)), ((), ()))
            pair_of = right[g].reshape(2 * LANES, pairs)
            both = lax.dot_general(green_split[rows, :pairs], pair_of, dims, preferred_element_type=jnp.float32)
            cross = lax.dot_general(green_split[rows, pairs:], right[g, 0], dims, preferred_element_type=jnp.float32)
            total = both[:, :LANES] + both[:, LANES:] + cross
            part[g, side, at] = total.reshape(2, share, LANES)

        @pl.loop(0, half)
        def _(at):
            product(1 - core, at)

        part_copy(g).start()

        @pl.loop(0, half)
        def _(step):
            product(core, lax.rem(hop + 1 + step, half))

    def add_partner(g):
        part_copy(g).wait()
        for d in list(range(1, half)) + [0]:
            at = peer_hop(d)
            part[g, core, at] = part[g, core, at] + first[g, at]
            if d:
                sum_copy(g, d).start()

    def cap(g):
        total = part[g, core, hop]
        for d in range(1, half):
            sum_copy(g, d).wait()
            total = total + second[g, d - 1]
        columns = slice(g * LANES, (g + 1) * LANES)
        value = 2.0 * jnp.tanh((total - mean_turned[:, columns][:, None, :]) / 2.0)
        capped[g, core, hop] = value
        share_ref[:, :, columns] = value
        for d in range(1, half):
            peer_copy(g, d).start()
        own_copy(g).start()

    def hand_on(g):
        for d in range(1, half):
            peer_copy(g, d).wait()
            pass_copy(g, d).start()

    def finish(g):
        own_copy(g).wait()
        for d in range(1, half):
            pass_copy(g, d).wait()
        if g >= early:
            capped_copy(g).start()

    def early_copy(t):
        return pltpu.make_async_copy(staging.at[t % slots], early_out.at[t // 2, t % 2], early_sem.at[t % slots])

    def early_product(j):
        cut = 256 if pairs % 256 == 0 else LANES
        noise_copy(j).wait()
        for c in range(2):
            at = slice(c * share, (c + 1) * share)
            if c == 0:
                turned = pltpu.roll(noise_tile[...], turn, 1)
            for g in range(early):
                value = capped[g, j % 2, j // 2, c]
                value = turned[:, g * LANES : (g + 1) * LANES] - value if c == 0 else -value
                high, low = split(value)
                left[at, 2 * g * LANES : (2 * g + 1) * LANES] = high
                left[at, (2 * g + 1) * LANES : (2 * g + 2) * LANES] = high
                left[at, (2 * early + g) * LANES : (2 * early + g + 1) * LANES] = low
        if j + 1 < n_pair:
            noise_copy(j + 1).start()
        for t in range(2 * j, 2 * j + 2):
            if t >= slots:
                early_copy(t - slots).wait()

        @pl.loop(0, pairs // cut)
        def _(step):
            column = pl.ds(pl.multiple_of(step * cut, cut), cut)
            total = jnp.dot(left[...], stacked(right, early, column), preferred_element_type=jnp.float32)
            for c in range(2):
                staging[(2 * j + c) % slots, :, column] = total[c * share : (c + 1) * share]

        for t in range(2 * j, 2 * j + 2):
            early_copy(t).start()

    def exchange(g, between):
        add_partner(g)
        between(0)
        cap(g)
        between(1)
        hand_on(g)
        between(2)
        finish(g)

    per_step = pl.cdiv(n_pair, 4)

    def some(step):
        for j in range(step * per_step, min((step + 1) * per_step, n_pair)):
            early_product(j)

    for g in range(granules):
        products(g)
        exchange(g, some if g == early else lambda step: None)
        if g == early:
            some(3)
    for k in range(chunks - own):
        ring(k).wait_send()
    for g in range(early, granules):
        chol_copy(g).wait()
        capped_copy(g).wait()
    for t in range(max(2 * n_pair - slots, 0), 2 * n_pair):
        early_copy(t).wait()


def bias(chol, green, noise, mean, n_field, n_pair):
    block, pairs = chol.shape
    walkers = green.shape[1]
    fields = block * n_field
    share, half = walkers // n_pair, n_pair // 2
    granules, chunks = fields // LANES, fields // math.gcd(block, LANES)
    late = 2
    early = granules - late
    dma = pltpu.SemaphoreType.DMA
    several = (granules, max(half - 1, 1))
    piece = (2, share, LANES)
    return pl.pallas_call(
        functools.partial(bias_kernel, n_field, n_pair, late),
        in_specs=[pl.BlockSpec(memory_space=pl.ANY)] * 3 + [pl.BlockSpec(memory_space=pltpu.VMEM)],
        out_specs=[pl.BlockSpec(memory_space=pltpu.VMEM)] + [pl.BlockSpec(memory_space=pl.ANY)] * 3,
        out_shape=[
            jax.ShapeDtypeStruct((2, share, fields), jnp.float32),
            jax.ShapeDtypeStruct((late, 2, LANES, pairs), jnp.bfloat16),
            jax.ShapeDtypeStruct((late, 2, half) + piece, jnp.float32),
            jax.ShapeDtypeStruct((n_pair, 2, share, pairs), jnp.float32),
        ],
        scratch_shapes=[
            pltpu.VMEM((fields, pairs), jnp.float32),
            pltpu.VMEM((2 * walkers, 2 * pairs), jnp.bfloat16),
            pltpu.VMEM((4, share, pairs), jnp.float32),
            pltpu.VMEM((granules, 2, LANES, pairs), jnp.bfloat16),
            pltpu.VMEM((granules, 2, half) + piece, jnp.float32),
            pltpu.VMEM((granules, half) + piece, jnp.float32),
            pltpu.VMEM(several + piece, jnp.float32),
            pltpu.VMEM((granules, 2, half) + piece, jnp.float32),
            pltpu.VMEM((2, fields), jnp.float32),
            pltpu.VMEM((share, fields), jnp.float32),
            pltpu.VMEM((2 * share, 3 * early * LANES), jnp.bfloat16),
            dma((chunks,)), dma((chunks,)),
            dma((granules,)), dma((granules,)),
            dma(several), dma(several),
            dma((granules,)), dma((granules,)),
            dma(several), dma(several),
            dma(several), dma(several),
            dma, dma((4,)), dma((late,)), dma((late,)), dma, dma((4,)),
        ],
        compiler_params=pltpu.CompilerParams(collective_id=0, has_side_effects=True, vmem_limit_bytes=63 << 20),
    )(chol, green, noise, mean)


def operator_kernel(scale, n_field, capped_ref, noise_ref, chol_ref, early_ref, share_ref, out_ref, turned_ref, left):
    rows, fields = noise_ref.shape
    late, _, _, pairs = chol_ref.shape
    before = fields - late * LANES
    cut = 256 if pairs % 256 == 0 else LANES
    ahead = lax.axis_index("field") * (fields // n_field)

    @pl.when(pl.program_id(0) == 0)
    def _():
        for c in range(2):
            turned_ref[c] = pltpu.roll(share_ref[c], ahead, 1)

    noise = pltpu.roll(noise_ref[...], lax.rem(fields - ahead, fields), 1)
    for g in range(late):
        for c in range(2):
            value = capped_ref[g, 0, 0, c]
            value = noise[:, before + g * LANES : before + (g + 1) * LANES] - value if c == 0 else -value
            high, low = split(value)
            at = slice(c * rows, (c + 1) * rows)
            left[at, 2 * g * LANES : (2 * g + 1) * LANES] = high
            left[at, (2 * g + 1) * LANES : (2 * g + 2) * LANES] = high
            left[at, (2 * late + g) * LANES : (2 * late + g + 1) * LANES] = low

    for step in range(pairs // cut):
        column = slice(step * cut, (step + 1) * cut)
        total = jnp.dot(left[...], stacked(chol_ref, late, column), preferred_element_type=jnp.float32)
        for c in range(2):
            out_ref[:, c, column] = scale * (early_ref[0, c, :, column] + total[c * rows : (c + 1) * rows])


def operator(capped, noise, chol, early, share, n_field, all_pairs):
    walkers, fields = noise.shape
    late, _, half, _, rows, _ = capped.shape
    pairs = chol.shape[3]
    scale = math.sqrt(all_pairs / fields)
    return pl.pallas_call(
        functools.partial(operator_kernel, scale, n_field),
        grid=(walkers // rows,),
        in_specs=[
            pl.BlockSpec((late, 1, 1, 2, rows, LANES), lambda i: (0, i % 2, i // 2, 0, 0, 0)),
            pl.BlockSpec((rows, fields), lambda i: (i, 0)),
            pl.BlockSpec((late, 2, LANES, pairs), lambda i: (0, 0, 0, 0)),
            pl.BlockSpec((1, 2, rows, pairs), lambda i: (i, 0, 0, 0)),
            pl.BlockSpec((2, rows, fields), lambda i: (0, 0, 0)),
        ],
        out_specs=[
            pl.BlockSpec((rows, 2, pairs), lambda i: (i, 0, 0)),
            pl.BlockSpec((2, rows, fields), lambda i: (0, 0, 0)),
        ],
        out_shape=[
            jax.ShapeDtypeStruct((walkers, 2, pairs), jnp.float32),
            jax.ShapeDtypeStruct((2, rows, fields), jnp.float32),
        ],
        scratch_shapes=[
            pltpu.VMEM((2 * rows, 3 * late * LANES), jnp.bfloat16),
        ],
        compiler_params=pltpu.CompilerParams(vmem_limit_bytes=60 << 20),
    )(capped, noise, chol, early, share)


def per_device(n_field, n_pair, cholesky_tensor, green_function, mean_field, field_noise):
    share, chol, capped, early = bias(cholesky_tensor, green_function, field_noise, mean_field, n_field, n_pair)
    all_pairs = cholesky_tensor.shape[1] * n_pair
    one_body, turned = operator(capped, field_noise, chol, early, share, n_field, all_pairs)
    return turned, one_body


def solution(mesh):
    return jax.shard_map(
        functools.partial(per_device, mesh.shape["field"], mesh.shape["pair"]),
        mesh=mesh,
        in_specs=(
            P(("grp", "field"), "pair"),
            P(None, ("grp", "field"), "pair"),
            P(None, "grp"),
            P(("grp", "field"), None),
        ),
        out_specs=(P(None, ("grp", "field", "pair"), None), P(("grp", "field"), None, "pair")),
        check_vma=False,
    )
```

```python
import functools
import math

import jax
import jax.numpy as jnp
from jax import lax
from jax.experimental import pallas as pl
from jax.experimental.pallas import tpu as pltpu
from jax.sharding import PartitionSpec as P

LANES = 128


def split(x):
    high = x.astype(jnp.bfloat16)
    return high, (x - high.astype(jnp.float32)).astype(jnp.bfloat16)


MESH = pl.DeviceIdType.MESH


def stacked(right, granules, column):
    wide = right[:granules, :, :, column]
    high = right[:granules, 0, :, column]
    return jnp.concatenate([wide.reshape(-1, wide.shape[3]), high.reshape(-1, high.shape[2])], axis=0)


def bias_kernel(
    n_field, n_pair, late, chol_in, green, noise, mean_ref, share_ref, chol_out, capped_out, early_out,
    stack, green_split, staging, right, part, first, second, capped, mean_turned, noise_tile, left,
    ring_send, ring_recv, part_send, part_recv, sum_send, sum_recv, own_send, own_recv,
    peer_send, peer_recv, pass_send, pass_recv, load_sem, green_sem, chol_sem, capped_sem, noise_sem, early_sem,
):
    fields, pairs = stack.shape
    share, slots = share_ref.shape[1], staging.shape[0]
    block = chol_in.shape[0]
    chunk = math.gcd(block, LANES)
    chunks, own = fields // chunk, block // chunk
    granules, per_granule = fields // LANES, LANES // chunk
    half = n_pair // 2
    me_field, me_pair = lax.axis_index("field"), lax.axis_index("pair")
    left_id = {"field": lax.rem(me_field + n_field - 1, n_field)}
    right_id = {"field": lax.rem(me_field + 1, n_field)}
    core, hop = lax.rem(me_pair, 2), me_pair // 2
    partner_id = {"pair": me_pair + 1 - 2 * core}

    def peer_hop(d):
        return lax.rem(hop + d, half)

    def peer_id(d):
        return {"pair": 2 * peer_hop(d) + core}

    barrier = pltpu.get_barrier_semaphore()
    others = [left_id, right_id, partner_id] + [peer_id(d) for d in range(1, half)]
    for other in others:
        pl.semaphore_signal(barrier, inc=1, device_id=other, device_id_type=MESH)
    pl.semaphore_wait(barrier, len(others))

    def remote(source, target, send, recv, device):
        return pltpu.make_async_remote_copy(
            src_ref=source, dst_ref=target, send_sem=send, recv_sem=recv, device_id=device, device_id_type=MESH
        )

    def ring(k):
        source = chol_in.at[pl.ds(k * chunk, chunk)] if k < own else stack.at[pl.ds(k * chunk, chunk)]
        target = stack.at[pl.ds((k + own) * chunk, chunk)]
        return remote(source, target, ring_send.at[k], ring_recv.at[k + own], left_id)

    for k in range(min(own, chunks - own)):
        ring(k).start()
    load = pltpu.make_async_copy(chol_in, stack.at[pl.ds(0, block)], load_sem)
    load.start()
    early = granules - late
    turn = lax.rem(fields - me_field * block, fields)

    def noise_copy(j):
        return pltpu.make_async_copy(noise.at[pl.ds(j * share, share)], noise_tile, noise_sem)

    noise_copy(0).start()
    mean_turned[...] = pltpu.roll(mean_ref[...], turn, 1)

    def fetch(t):
        j, c = t // 2, t % 2
        return pltpu.make_async_copy(green.at[c, pl.ds(j * share, share)], staging.at[t % slots], green_sem.at[t % slots])

    for t in range(slots - 1):
        fetch(t).start()
    for t in range(2 * n_pair):
        if t + slots - 1 < 2 * n_pair:
            fetch(t + slots - 1).start()
        fetch(t).wait()

        @pl.loop(0, share // 16)
        def _(step):
            at = pl.multiple_of(step * 16, 16)
            high, low = split(staging[t % slots, pl.ds(at, 16), :])
            into = pl.multiple_of(t * share + at, 16)
            green_split[pl.ds(into, 16), :pairs] = high
            green_split[pl.ds(into, 16), pairs:] = low

    load.wait()

    def part_copy(g, at):
        return remote(part.at[g, 1 - core, at], first.at[g, at], part_send.at[g, at], part_recv.at[g, at], partner_id)

    def sum_copy(g, d, c):
        source, at = part.at[g, core, peer_hop(d), c], (g, d - 1, c)
        return remote(source, second.at[at], sum_send.at[at], sum_recv.at[at], peer_id(d))

    def own_copy(g):
        at = capped.at[g, core, hop]
        return remote(at, at, own_send.at[g], own_recv.at[g], partner_id)

    def peer_copy(g, d, c):
        at, sem = capped.at[g, core, hop, c], (g, d - 1, c)
        return remote(at, at, peer_send.at[sem], peer_recv.at[sem], peer_id(d))

    def pass_copy(g, d, c):
        at, sem = capped.at[g, core, peer_hop(half - d), c], (g, d - 1, c)
        return remote(at, at, pass_send.at[sem], pass_recv.at[sem], partner_id)

    def chol_copy(g):
        return pltpu.make_async_copy(right.at[g], chol_out.at[g - early], chol_sem.at[g - early])

    def capped_copy(g):
        return pltpu.make_async_copy(capped.at[g], capped_out.at[g - early], capped_sem.at[g - early])

    def pump(end):
        while passed[0] < min(end, chunks):
            k = passed[0]
            ring(k - own).wait_recv()
            if k + own < chunks:
                ring(k).start()
            passed[0] += 1

    passed = [own]

    def products(g):
        pump((g + 1) * per_granule)
        step_rows = 32
        for at in range(0, LANES, step_rows):
            high, low = split(stack[g * LANES + at : g * LANES + at + step_rows, :])
            right[g, 0, at : at + step_rows, :] = high
            right[g, 1, at : at + step_rows, :] = low
        if g >= early:
            chol_copy(g).start()

        def product(side, at):
            rows = pl.ds(pl.multiple_of((2 * at + side) * 2 * share, 16), 2 * share)
            dims = (((1,), (1,)), ((), ()))
            pair_of = right[g].reshape(2 * LANES, pairs)
            both = lax.dot_general(green_split[rows, :pairs], pair_of, dims, preferred_element_type=jnp.float32)
            cross = lax.dot_general(green_split[rows, pairs:], right[g, 0], dims, preferred_element_type=jnp.float32)
            total = both[:, :LANES] + both[:, LANES:] + cross
            part[g, side, at] = total.reshape(2, share, LANES)

        @pl.loop(0, half)
        def _(step):
            at = peer_hop(step + 1)
            product(1 - core, at)
            part_copy(g, at).start()

        @pl.loop(0, half)
        def _(step):
            at = peer_hop(step + 1)
            product(core, at)
            part_copy(g, at).wait()
            part[g, core, at] = part[g, core, at] + first[g, at]

            @pl.when(step < half - 1)
            def _():
                for c in range(2):
                    sum_copy(g, step + 1, c).start()

    def cap(g):
        columns = slice(g * LANES, (g + 1) * LANES)
        for c in range(2):
            total = part[g, core, hop, c]
            for d in range(1, half):
                sum_copy(g, d, c).wait()
                total = total + second[g, d - 1, c]
            value = 2.0 * jnp.tanh((total - mean_turned[c : c + 1, columns]) / 2.0)
            capped[g, core, hop, c] = value
            share_ref[c, :, columns] = value
            for d in range(1, half):
                peer_copy(g, d, c).start()
        own_copy(g).start()

    def hand_on(g):
        for c in range(2):
            for d in range(1, half):
                peer_copy(g, d, c).wait()
                pass_copy(g, d, c).start()

    def finish(g):
        own_copy(g).wait()
        for c in range(2):
            for d in range(1, half):
                pass_copy(g, d, c).wait()
        if g >= early:
            capped_copy(g).start()

    def early_copy(t):
        return pltpu.make_async_copy(staging.at[t % slots], early_out.at[t // 2, t % 2], early_sem.at[t % slots])

    def early_product(j):
        cut = 256 if pairs % 256 == 0 else LANES
        noise_copy(j).wait()
        for c in range(2):
            at = slice(c * share, (c + 1) * share)
            if c == 0:
                turned = pltpu.roll(noise_tile[...], turn, 1)
            for g in range(early):
                value = capped[g, j % 2, j // 2, c]
                value = turned[:, g * LANES : (g + 1) * LANES] - value if c == 0 else -value
                high, low = split(value)
                left[at, 2 * g * LANES : (2 * g + 1) * LANES] = high
                left[at, (2 * g + 1) * LANES : (2 * g + 2) * LANES] = high
                left[at, (2 * early + g) * LANES : (2 * early + g + 1) * LANES] = low
        if j + 1 < n_pair:
            noise_copy(j + 1).start()
        for t in range(2 * j, 2 * j + 2):
            if t >= slots:
                early_copy(t - slots).wait()

        @pl.loop(0, pairs // cut)
        def _(step):
            column = pl.ds(pl.multiple_of(step * cut, cut), cut)
            total = jnp.dot(left[...], stacked(right, early, column), preferred_element_type=jnp.float32)
            for c in range(2):
                staging[(2 * j + c) % slots, :, column] = total[c * share : (c + 1) * share]

        for t in range(2 * j, 2 * j + 2):
            early_copy(t).start()

    per_step = pl.cdiv(n_pair, 4)

    def some(step):
        for j in range(step * per_step, min((step + 1) * per_step, n_pair)):
            early_product(j)

    products(0)
    for g in range(1, granules):
        products(g)
        if g == 1:
            cap(0)
            cap(1)
            pump(2 * per_granule + per_granule // 2)
            hand_on(0)
            hand_on(1)
            finish(0)
            continue
        finish(g - 1)
        if g == early:
            some(0)
        cap(g)
        if g == early:
            some(1)
        elif g < early:
            pump((g + 1) * per_granule + per_granule // 2)
        hand_on(g)
        if g == early:
            some(2)
            some(3)
    finish(granules - 1)
    for k in range(chunks - own):
        ring(k).wait_send()
    for g in range(early, granules):
        chol_copy(g).wait()
        capped_copy(g).wait()
    for t in range(max(2 * n_pair - slots, 0), 2 * n_pair):
        early_copy(t).wait()


def bias(chol, green, noise, mean, n_field, n_pair):
    block, pairs = chol.shape
    walkers = green.shape[1]
    fields = block * n_field
    share, half = walkers // n_pair, n_pair // 2
    granules, chunks = fields // LANES, fields // math.gcd(block, LANES)
    late = 2
    early = granules - late
    dma = pltpu.SemaphoreType.DMA
    several = (granules, max(half - 1, 1), 2)
    piece = (2, share, LANES)
    return pl.pallas_call(
        functools.partial(bias_kernel, n_field, n_pair, late),
        in_specs=[pl.BlockSpec(memory_space=pl.ANY)] * 3 + [pl.BlockSpec(memory_space=pltpu.VMEM)],
        out_specs=[pl.BlockSpec(memory_space=pltpu.VMEM)] + [pl.BlockSpec(memory_space=pl.ANY)] * 3,
        out_shape=[
            jax.ShapeDtypeStruct((2, share, fields), jnp.float32),
            jax.ShapeDtypeStruct((late, 2, LANES, pairs), jnp.bfloat16),
            jax.ShapeDtypeStruct((late, 2, half) + piece, jnp.float32),
            jax.ShapeDtypeStruct((n_pair, 2, share, pairs), jnp.float32),
        ],
        scratch_shapes=[
            pltpu.VMEM((fields, pairs), jnp.float32),
            pltpu.VMEM((2 * walkers, 2 * pairs), jnp.bfloat16),
            pltpu.VMEM((4, share, pairs), jnp.float32),
            pltpu.VMEM((granules, 2, LANES, pairs), jnp.bfloat16),
            pltpu.VMEM((granules, 2, half) + piece, jnp.float32),
            pltpu.VMEM((granules, half) + piece, jnp.float32),
            pltpu.VMEM(several[:2] + piece, jnp.float32),
            pltpu.VMEM((granules, 2, half) + piece, jnp.float32),
            pltpu.VMEM((2, fields), jnp.float32),
            pltpu.VMEM((share, fields), jnp.float32),
            pltpu.VMEM((2 * share, 3 * early * LANES), jnp.bfloat16),
            dma((chunks,)), dma((chunks,)),
            dma((granules, half)), dma((granules, half)),
            dma(several), dma(several),
            dma((granules,)), dma((granules,)),
            dma(several), dma(several),
            dma(several), dma(several),
            dma, dma((4,)), dma((late,)), dma((late,)), dma, dma((4,)),
        ],
        compiler_params=pltpu.CompilerParams(collective_id=0, has_side_effects=True, vmem_limit_bytes=63 << 20),
    )(chol, green, noise, mean)


def operator_kernel(scale, n_field, capped_ref, noise_ref, chol_ref, early_ref, share_ref, out_ref, turned_ref, left):
    rows, fields = noise_ref.shape
    late, _, _, pairs = chol_ref.shape
    before = fields - late * LANES
    cut = 256 if pairs % 256 == 0 else LANES
    ahead = lax.axis_index("field") * (fields // n_field)

    @pl.when(pl.program_id(0) == 0)
    def _():
        for c in range(2):
            turned_ref[c] = pltpu.roll(share_ref[c], ahead, 1)

    noise = pltpu.roll(noise_ref[...], lax.rem(fields - ahead, fields), 1)
    for g in range(late):
        for c in range(2):
            value = capped_ref[g, 0, 0, c]
            value = noise[:, before + g * LANES : before + (g + 1) * LANES] - value if c == 0 else -value
            high, low = split(value)
            at = slice(c * rows, (c + 1) * rows)
            left[at, 2 * g * LANES : (2 * g + 1) * LANES] = high
            left[at, (2 * g + 1) * LANES : (2 * g + 2) * LANES] = high
            left[at, (2 * late + g) * LANES : (2 * late + g + 1) * LANES] = low

    for step in range(pairs // cut):
        column = slice(step * cut, (step + 1) * cut)
        total = jnp.dot(left[...], stacked(chol_ref, late, column), preferred_element_type=jnp.float32)
        for c in range(2):
            out_ref[:, c, column] = scale * (early_ref[0, c, :, column] + total[c * rows : (c + 1) * rows])


def operator(capped, noise, chol, early, share, n_field, all_pairs):
    walkers, fields = noise.shape
    late, _, half, _, rows, _ = capped.shape
    pairs = chol.shape[3]
    scale = math.sqrt(all_pairs / fields)
    return pl.pallas_call(
        functools.partial(operator_kernel, scale, n_field),
        grid=(walkers // rows,),
        in_specs=[
            pl.BlockSpec((late, 1, 1, 2, rows, LANES), lambda i: (0, i % 2, i // 2, 0, 0, 0)),
            pl.BlockSpec((rows, fields), lambda i: (i, 0)),
            pl.BlockSpec((late, 2, LANES, pairs), lambda i: (0, 0, 0, 0)),
            pl.BlockSpec((1, 2, rows, pairs), lambda i: (i, 0, 0, 0)),
            pl.BlockSpec((2, rows, fields), lambda i: (0, 0, 0)),
        ],
        out_specs=[
            pl.BlockSpec((rows, 2, pairs), lambda i: (i, 0, 0)),
            pl.BlockSpec((2, rows, fields), lambda i: (0, 0, 0)),
        ],
        out_shape=[
            jax.ShapeDtypeStruct((walkers, 2, pairs), jnp.float32),
            jax.ShapeDtypeStruct((2, rows, fields), jnp.float32),
        ],
        scratch_shapes=[
            pltpu.VMEM((2 * rows, 3 * late * LANES), jnp.bfloat16),
        ],
        compiler_params=pltpu.CompilerParams(vmem_limit_bytes=60 << 20),
    )(capped, noise, chol, early, share)


def per_device(n_field, n_pair, cholesky_tensor, green_function, mean_field, field_noise):
    share, chol, capped, early = bias(cholesky_tensor, green_function, field_noise, mean_field, n_field, n_pair)
    all_pairs = cholesky_tensor.shape[1] * n_pair
    one_body, turned = operator(capped, field_noise, chol, early, share, n_field, all_pairs)
    return turned, one_body


def solution(mesh):
    return jax.shard_map(
        functools.partial(per_device, mesh.shape["field"], mesh.shape["pair"]),
        mesh=mesh,
        in_specs=(
            P(("grp", "field"), "pair"),
            P(None, ("grp", "field"), "pair"),
            P(None, "grp"),
            P(("grp", "field"), None),
        ),
        out_specs=(P(None, ("grp", "field", "pair"), None), P(("grp", "field"), None, "pair")),
        check_vma=False,
    )
```

```python
import functools
import math

import jax
import jax.numpy as jnp
from jax import lax
from jax.experimental import pallas as pl
from jax.experimental.pallas import tpu as pltpu
from jax.sharding import PartitionSpec as P

LANES = 128


def split(x):
    high = x.astype(jnp.bfloat16)
    return high, (x - high.astype(jnp.float32)).astype(jnp.bfloat16)


MESH = pl.DeviceIdType.MESH


def stacked(right, granules, column):
    wide = right[:granules, :, :, column]
    high = right[:granules, 0, :, column]
    return jnp.concatenate([wide.reshape(-1, wide.shape[3]), high.reshape(-1, high.shape[2])], axis=0)


def bias_kernel(
    n_field, n_pair, late, chol_in, green, noise, mean_ref, share_ref, chol_out, capped_out, early_out,
    stack, green_split, staging, right, part, first, second, capped, mean_turned, noise_tile, left,
    ring_send, ring_recv, part_send, part_recv, sum_send, sum_recv, own_send, own_recv,
    peer_send, peer_recv, pass_send, pass_recv, load_sem, green_sem, chol_sem, capped_sem, noise_sem, early_sem,
):
    fields, pairs = stack.shape
    share, slots = share_ref.shape[1], staging.shape[0]
    block = chol_in.shape[0]
    chunk = math.gcd(block, LANES)
    chunks, own = fields // chunk, block // chunk
    granules, per_granule = fields // LANES, LANES // chunk
    half = n_pair // 2
    me_field, me_pair = lax.axis_index("field"), lax.axis_index("pair")
    left_id = {"field": lax.rem(me_field + n_field - 1, n_field)}
    right_id = {"field": lax.rem(me_field + 1, n_field)}
    core, hop = lax.rem(me_pair, 2), me_pair // 2
    partner_id = {"pair": me_pair + 1 - 2 * core}

    def peer_hop(d):
        return lax.rem(hop + d, half)

    def peer_id(d):
        return {"pair": 2 * peer_hop(d) + core}

    barrier = pltpu.get_barrier_semaphore()
    others = [left_id, right_id, partner_id] + [peer_id(d) for d in range(1, half)]
    for other in others:
        pl.semaphore_signal(barrier, inc=1, device_id=other, device_id_type=MESH)
    pl.semaphore_wait(barrier, len(others))

    def remote(source, target, send, recv, device):
        return pltpu.make_async_remote_copy(
            src_ref=source, dst_ref=target, send_sem=send, recv_sem=recv, device_id=device, device_id_type=MESH
        )

    def ring(k):
        source = chol_in.at[pl.ds(k * chunk, chunk)] if k < own else stack.at[pl.ds(k * chunk, chunk)]
        target = stack.at[pl.ds((k + own) * chunk, chunk)]
        return remote(source, target, ring_send.at[k], ring_recv.at[k + own], left_id)

    for k in range(min(own, chunks - own)):
        ring(k).start()
    load = pltpu.make_async_copy(chol_in, stack.at[pl.ds(0, block)], load_sem)
    load.start()
    early = granules - late
    turn = lax.rem(fields - me_field * block, fields)

    def noise_copy(j):
        return pltpu.make_async_copy(noise.at[pl.ds(j * share, share)], noise_tile, noise_sem)

    noise_copy(0).start()
    mean_turned[...] = pltpu.roll(mean_ref[...], turn, 1)

    def fetch(t):
        j, c = t // 2, t % 2
        return pltpu.make_async_copy(green.at[c, pl.ds(j * share, share)], staging.at[t % slots], green_sem.at[t % slots])

    for t in range(slots - 1):
        fetch(t).start()
    for t in range(2 * n_pair):
        if t + slots - 1 < 2 * n_pair:
            fetch(t + slots - 1).start()
        fetch(t).wait()

        @pl.loop(0, share // 16)
        def _(step):
            at = pl.multiple_of(step * 16, 16)
            high, low = split(staging[t % slots, pl.ds(at, 16), :])
            into = pl.multiple_of(t * share + at, 16)
            green_split[pl.ds(into, 16), :pairs] = high
            green_split[pl.ds(into, 16), pairs:] = low

    load.wait()

    def part_copy(g, at):
        return remote(part.at[g, 1 - core, at], first.at[g, at], part_send.at[g, at], part_recv.at[g, at], partner_id)

    def sum_copy(g, d, c):
        source, at = part.at[g, core, peer_hop(d), c], (g, d - 1, c)
        return remote(source, second.at[at], sum_send.at[at], sum_recv.at[at], peer_id(d))

    def own_copy(g):
        at = capped.at[g, core, hop]
        return remote(at, at, own_send.at[g], own_recv.at[g], partner_id)

    def peer_copy(g, d, c):
        at, sem = capped.at[g, core, hop, c], (g, d - 1, c)
        return remote(at, at, peer_send.at[sem], peer_recv.at[sem], peer_id(d))

    def pass_copy(g, d, c):
        at, sem = capped.at[g, core, peer_hop(half - d), c], (g, d - 1, c)
        return remote(at, at, pass_send.at[sem], pass_recv.at[sem], partner_id)

    def chol_copy(g):
        return pltpu.make_async_copy(right.at[g], chol_out.at[g - early], chol_sem.at[g - early])

    def capped_copy(g):
        return pltpu.make_async_copy(capped.at[g], capped_out.at[g - early], capped_sem.at[g - early])

    def pump(end):
        while passed[0] < min(end, chunks):
            k = passed[0]
            ring(k - own).wait_recv()
            if k + own < chunks:
                ring(k).start()
            passed[0] += 1

    passed = [own]

    def products(g):
        pump((g + 1) * per_granule)
        step_rows = 32
        for at in range(0, LANES, step_rows):
            high, low = split(stack[g * LANES + at : g * LANES + at + step_rows, :])
            right[g, 0, at : at + step_rows, :] = high
            right[g, 1, at : at + step_rows, :] = low
        if g >= early:
            chol_copy(g).start()

        def product(side, at):
            rows = pl.ds(pl.multiple_of((2 * at + side) * 2 * share, 16), 2 * share)
            dims = (((1,), (1,)), ((), ()))
            pair_of = right[g].reshape(2 * LANES, pairs)
            both = lax.dot_general(green_split[rows, :pairs], pair_of, dims, preferred_element_type=jnp.float32)
            cross = lax.dot_general(green_split[rows, pairs:], right[g, 0], dims, preferred_element_type=jnp.float32)
            total = both[:, :LANES] + both[:, LANES:] + cross
            part[g, side, at] = total.reshape(2, share, LANES)

        @pl.loop(0, half)
        def _(step):
            at = peer_hop(step + 1)
            product(1 - core, at)
            part_copy(g, at).start()

        @pl.loop(0, half)
        def _(step):
            at = peer_hop(step + 1)
            product(core, at)
            part_copy(g, at).wait()
            part[g, core, at] = part[g, core, at] + first[g, at]

            @pl.when(step < half - 1)
            def _():
                for c in range(2):
                    sum_copy(g, step + 1, c).start()

    def cap(g):
        columns = slice(g * LANES, (g + 1) * LANES)
        for c in range(2):
            total = part[g, core, hop, c]
            for d in range(1, half):
                sum_copy(g, d, c).wait()
                total = total + second[g, d - 1, c]
            value = 2.0 * jnp.tanh((total - mean_turned[c : c + 1, columns]) / 2.0)
            capped[g, core, hop, c] = value
            share_ref[c, :, columns] = value
            for d in range(1, half):
                peer_copy(g, d, c).start()
        own_copy(g).start()

    def hand_on(g):
        for c in range(2):
            for d in range(1, half):
                peer_copy(g, d, c).wait()
                pass_copy(g, d, c).start()

    def finish(g):
        own_copy(g).wait()
        for c in range(2):
            for d in range(1, half):
                pass_copy(g, d, c).wait()
        if g >= early:
            capped_copy(g).start()

    def early_copy(t):
        return pltpu.make_async_copy(staging.at[t % slots], early_out.at[t // 2, t % 2], early_sem.at[t % slots])

    def early_product(j):
        cut = 256 if pairs % 256 == 0 else LANES
        noise_copy(j).wait()
        for c in range(2):
            at = slice(c * share, (c + 1) * share)
            if c == 0:
                turned = pltpu.roll(noise_tile[...], turn, 1)
            for g in range(early):
                value = capped[g, j % 2, j // 2, c]
                value = turned[:, g * LANES : (g + 1) * LANES] - value if c == 0 else -value
                high, low = split(value)
                left[at, 2 * g * LANES : (2 * g + 1) * LANES] = high
                left[at, (2 * g + 1) * LANES : (2 * g + 2) * LANES] = high
                left[at, (2 * early + g) * LANES : (2 * early + g + 1) * LANES] = low
        if j + 1 < n_pair:
            noise_copy(j + 1).start()
        for t in range(2 * j, 2 * j + 2):
            if t >= slots:
                early_copy(t - slots).wait()

        @pl.loop(0, pairs // cut)
        def _(step):
            column = pl.ds(pl.multiple_of(step * cut, cut), cut)
            total = jnp.dot(left[...], stacked(right, early, column), preferred_element_type=jnp.float32)
            for c in range(2):
                staging[(2 * j + c) % slots, :, column] = total[c * share : (c + 1) * share]

        for t in range(2 * j, 2 * j + 2):
            early_copy(t).start()

    per_step = pl.cdiv(n_pair, 4)

    def some(step):
        for j in range(step * per_step, min((step + 1) * per_step, n_pair)):
            early_product(j)

    products(0)
    for g in range(1, granules):
        products(g)
        if g == 1:
            cap(0)
            cap(1)
            pump(2 * per_granule + per_granule // 2)
            hand_on(0)
            hand_on(1)
            finish(0)
            continue
        if g > early:
            some(2 * (g - early))
        finish(g - 1)
        if g == early:
            some(0)
        cap(g)
        if g >= early:
            some(2 * (g - early) + 1)
        else:
            pump((g + 1) * per_granule + per_granule // 2)
        hand_on(g)
    finish(granules - 1)
    for k in range(chunks - own):
        ring(k).wait_send()
    for g in range(early, granules):
        chol_copy(g).wait()
        capped_copy(g).wait()
    for t in range(max(2 * n_pair - slots, 0), 2 * n_pair):
        early_copy(t).wait()


def bias(chol, green, noise, mean, n_field, n_pair):
    block, pairs = chol.shape
    walkers = green.shape[1]
    fields = block * n_field
    share, half = walkers // n_pair, n_pair // 2
    granules, chunks = fields // LANES, fields // math.gcd(block, LANES)
    late = 2
    early = granules - late
    dma = pltpu.SemaphoreType.DMA
    several = (granules, max(half - 1, 1), 2)
    piece = (2, share, LANES)
    return pl.pallas_call(
        functools.partial(bias_kernel, n_field, n_pair, late),
        in_specs=[pl.BlockSpec(memory_space=pl.ANY)] * 3 + [pl.BlockSpec(memory_space=pltpu.VMEM)],
        out_specs=[pl.BlockSpec(memory_space=pltpu.VMEM)] + [pl.BlockSpec(memory_space=pl.ANY)] * 3,
        out_shape=[
            jax.ShapeDtypeStruct((2, share, fields), jnp.float32),
            jax.ShapeDtypeStruct((late, 2, LANES, pairs), jnp.bfloat16),
            jax.ShapeDtypeStruct((late, 2, half) + piece, jnp.float32),
            jax.ShapeDtypeStruct((n_pair, 2, share, pairs), jnp.float32),
        ],
        scratch_shapes=[
            pltpu.VMEM((fields, pairs), jnp.float32),
            pltpu.VMEM((2 * walkers, 2 * pairs), jnp.bfloat16),
            pltpu.VMEM((4, share, pairs), jnp.float32),
            pltpu.VMEM((granules, 2, LANES, pairs), jnp.bfloat16),
            pltpu.VMEM((granules, 2, half) + piece, jnp.float32),
            pltpu.VMEM((granules, half) + piece, jnp.float32),
            pltpu.VMEM(several[:2] + piece, jnp.float32),
            pltpu.VMEM((granules, 2, half) + piece, jnp.float32),
            pltpu.VMEM((2, fields), jnp.float32),
            pltpu.VMEM((share, fields), jnp.float32),
            pltpu.VMEM((2 * share, 3 * early * LANES), jnp.bfloat16),
            dma((chunks,)), dma((chunks,)),
            dma((granules, half)), dma((granules, half)),
            dma(several), dma(several),
            dma((granules,)), dma((granules,)),
            dma(several), dma(several),
            dma(several), dma(several),
            dma, dma((4,)), dma((late,)), dma((late,)), dma, dma((4,)),
        ],
        compiler_params=pltpu.CompilerParams(collective_id=0, has_side_effects=True, vmem_limit_bytes=63 << 20),
    )(chol, green, noise, mean)


def operator_kernel(scale, n_field, capped_ref, noise_ref, chol_ref, early_ref, share_ref, out_ref, turned_ref, left):
    rows, fields = noise_ref.shape
    late, _, _, pairs = chol_ref.shape
    before = fields - late * LANES
    cut = 256 if pairs % 256 == 0 else LANES
    ahead = lax.axis_index("field") * (fields // n_field)

    @pl.when(pl.program_id(0) == 0)
    def _():
        for c in range(2):
            turned_ref[c] = pltpu.roll(share_ref[c], ahead, 1)

    noise = pltpu.roll(noise_ref[...], lax.rem(fields - ahead, fields), 1)
    for g in range(late):
        for c in range(2):
            value = capped_ref[g, 0, 0, c]
            value = noise[:, before + g * LANES : before + (g + 1) * LANES] - value if c == 0 else -value
            high, low = split(value)
            at = slice(c * rows, (c + 1) * rows)
            left[at, 2 * g * LANES : (2 * g + 1) * LANES] = high
            left[at, (2 * g + 1) * LANES : (2 * g + 2) * LANES] = high
            left[at, (2 * late + g) * LANES : (2 * late + g + 1) * LANES] = low

    for step in range(pairs // cut):
        column = slice(step * cut, (step + 1) * cut)
        total = jnp.dot(left[...], stacked(chol_ref, late, column), preferred_element_type=jnp.float32)
        for c in range(2):
            out_ref[:, c, column] = scale * (early_ref[0, c, :, column] + total[c * rows : (c + 1) * rows])


def operator(capped, noise, chol, early, share, n_field, all_pairs):
    walkers, fields = noise.shape
    late, _, half, _, rows, _ = capped.shape
    pairs = chol.shape[3]
    scale = math.sqrt(all_pairs / fields)
    return pl.pallas_call(
        functools.partial(operator_kernel, scale, n_field),
        grid=(walkers // rows,),
        in_specs=[
            pl.BlockSpec((late, 1, 1, 2, rows, LANES), lambda i: (0, i % 2, i // 2, 0, 0, 0)),
            pl.BlockSpec((rows, fields), lambda i: (i, 0)),
            pl.BlockSpec((late, 2, LANES, pairs), lambda i: (0, 0, 0, 0)),
            pl.BlockSpec((1, 2, rows, pairs), lambda i: (i, 0, 0, 0)),
            pl.BlockSpec((2, rows, fields), lambda i: (0, 0, 0)),
        ],
        out_specs=[
            pl.BlockSpec((rows, 2, pairs), lambda i: (i, 0, 0)),
            pl.BlockSpec((2, rows, fields), lambda i: (0, 0, 0)),
        ],
        out_shape=[
            jax.ShapeDtypeStruct((walkers, 2, pairs), jnp.float32),
            jax.ShapeDtypeStruct((2, rows, fields), jnp.float32),
        ],
        scratch_shapes=[
            pltpu.VMEM((2 * rows, 3 * late * LANES), jnp.bfloat16),
        ],
        compiler_params=pltpu.CompilerParams(vmem_limit_bytes=60 << 20),
    )(capped, noise, chol, early, share)


def per_device(n_field, n_pair, cholesky_tensor, green_function, mean_field, field_noise):
    share, chol, capped, early = bias(cholesky_tensor, green_function, field_noise, mean_field, n_field, n_pair)
    all_pairs = cholesky_tensor.shape[1] * n_pair
    one_body, turned = operator(capped, field_noise, chol, early, share, n_field, all_pairs)
    return turned, one_body


def solution(mesh):
    return jax.shard_map(
        functools.partial(per_device, mesh.shape["field"], mesh.shape["pair"]),
        mesh=mesh,
        in_specs=(
            P(("grp", "field"), "pair"),
            P(None, ("grp", "field"), "pair"),
            P(None, "grp"),
            P(("grp", "field"), None),
        ),
        out_specs=(P(None, ("grp", "field", "pair"), None), P(("grp", "field"), None, "pair")),
        check_vma=False,
    )
```
